256 devices in a mesh: row: 16 (over z, y_lo), col: 16 (over y_hi, x, core).
Axes of the slice: x: 4, y: 4 (y_hi: 2, y_lo: 2; y = y_hi * 2 + y_lo), z: 8, core: 2. Of those that a mesh axis runs over, the one named last changes fastest.
Arguments:
- panels: bfloat16 [32, 32, 128, 128], P('row', 'col'), may hold values from -0.26367188 to 0.26367188
- obs_of: int32 [32, 32], replicated, may hold values from 0 to 63, as said below
- counts: int32 [32], replicated, may hold values from 16 to 32, as said below
- inv_var: float32 [64, 128], replicated, may hold values from 0.25 to 4
- pattern: int32 [32, 32], replicated, may hold values from 0 to 1, as said below
- prior: float32 [4096, 4096], P('row', 'col'), may hold values from -2 to 2
Outputs:
- information: float32 [4096, 4096], P('row', 'col')
The draws below stay inside these ranges and needn't reach their ends.
Inputs may be any that keep to these rules, and one draw needn't show every extreme that they name: The 32 entries of a row of obs_of are distinct. `counts`: some panel has all 32 slots live. pattern is 1 on the diagonal and 0 below it.
All inputs are finite; a program needn't handle non-finite values.
Results may differ from the reference program's by a relative error of at most 0.0011.
Values may be sent and summed in bfloat16 or wider, within the bound.
No kernel may reach another device: no remote copies, remote signals or barrier semaphores. Data moves between devices by JAX's collectives and lax.ppermute only.
A program may use at most 64 MiB of HBM per device.

```python
import math
import jax
import jax.numpy as jnp
from jax import lax

BS = 128
P_SIZE = 32
NB = 32
NOBS = 64


def draw_obs_of(key, part):
    row_keys = jax.random.split(jax.random.fold_in(key, 11), NB)
    rows_drawn = jax.vmap(lambda row_key: jax.random.permutation(row_key, NOBS)[:P_SIZE])(row_keys)
    return rows_drawn.astype(jnp.int32)


def draw_counts(key, part):
    key_vals = jax.random.fold_in(key, 21)
    key_full = jax.random.fold_in(key, 22)
    values = jax.random.randint(key_vals, (NB,), P_SIZE // 2, P_SIZE + 1)
    full_block = jax.random.randint(key_full, (), 0, NB)
    values = jnp.where(jnp.arange(NB) == full_block, P_SIZE, values)
    return values.astype(jnp.int32)


def draw_pattern(key, part):
    coin_flip = jax.random.randint(jax.random.fold_in(key, 31), (NB, NB), 0, 2)
    block_ids = jnp.arange(NB)
    diag_mask = block_ids[:, None] == block_ids[None, :]
    above_mask = block_ids[:, None] < block_ids[None, :]
    return jnp.where(diag_mask, 1, jnp.where(above_mask, coin_flip, 0)).astype(jnp.int32)


def block_levels(stream_key, extent, cuts, least, top_value):
    loudness = 1.0
    for axis_at, shards_of in cuts:
        steps = jax.random.uniform(jax.random.fold_in(jax.random.fold_in(stream_key, 6), axis_at), (shards_of,), jnp.float32, least / len(cuts), top_value / len(cuts))
        loudness = loudness * jnp.repeat(jnp.exp(steps), extent[axis_at] // shards_of).reshape((-1,) + (1,) * (len(extent) - 1 - axis_at))
    return loudness


def scatter_about(rng, extent, width, most, cuts=(), kind=jnp.bfloat16):
    result = jax.random.normal(rng, extent, jnp.float32) * width
    if len(cuts) > 0:
        result = block_levels(rng, extent, cuts, -0.22, 0.18) * result
    return jnp.clip(result, min=-most, max=most).astype(kind)


def setup_inputs(seed: int = 0) -> dict:
    splits = jax.random.split(jax.random.key(seed), 7)
    return {
        "panels": scatter_about(splits[0], (NB, P_SIZE, BS, BS), (0.5 / BS ** 0.5), 0.26367188, ((0, 16), (1, 16))),
        "obs_of": draw_obs_of(jax.random.fold_in(splits[6], 71), 0),
        "counts": draw_counts(jax.random.fold_in(splits[6], 71), 0),
        "inv_var": jnp.clip(jnp.exp(jax.random.uniform(splits[3], (NOBS, BS), jnp.float32, math.log(0.25), math.log(4.0))), 0.25, 4.0),
        "pattern": draw_pattern(jax.random.fold_in(splits[6], 71), 0),
        "prior": scatter_about(splits[5], (NB * BS, NB * BS), 0.3, 2.0, ((0, 16), (1, 16)), jnp.float32),
    }


def reference(panels, obs_of, counts, inv_var, pattern, prior):
    slot_ids = jnp.arange(P_SIZE, dtype=jnp.int32)
    live_slot = (slot_ids[None, :] < counts[:, None]).astype(jnp.float32)
    root_weight = jnp.sqrt(jnp.take(inv_var, obs_of, axis=0)) * live_slot[:, :, None]
    scaled = (panels.astype(jnp.float32) * root_weight[:, :, :, None]).astype(jnp.bfloat16)

    def pair_block(row_block, col_block):
        same_obs = obs_of[row_block][:, None] == obs_of[col_block][None, :]
        has_match = jnp.any(same_obs, axis=1)
        partner = lax.optimization_barrier(jnp.sum(jnp.where(same_obs, slot_ids[None, :], 0), axis=1)).astype(jnp.int32)
        picked = jnp.take(scaled[col_block], partner, axis=0).astype(jnp.float32)
        aligned = jnp.where(has_match[:, None, None], picked, jnp.zeros((), jnp.float32))
        return jnp.einsum('pax,pay->xy', scaled[row_block].astype(jnp.float32), aligned)

    def pair_step(carry, pair_index):
        row_block = pair_index // NB
        col_block = pair_index % NB
        pair_value = lax.cond(pattern[row_block, col_block] == 1, lambda: pair_block(row_block, col_block), lambda: jnp.zeros((BS, BS), jnp.float32))
        return (carry, pair_value)
    unused, blocks = lax.scan(pair_step, jnp.int32(0), jnp.arange(NB * NB, dtype=jnp.int32))
    upper_part = blocks.reshape(NB, NB, BS, BS)
    mirror_part = jnp.transpose(upper_part, (1, 0, 3, 2))
    block_ids = jnp.arange(NB, dtype=jnp.int32)
    lower_mask = (block_ids[:, None] > block_ids[None, :])[:, :, None, None]
    update = jnp.where(lower_mask, mirror_part, upper_part)
    return prior + jnp.transpose(update, (0, 2, 1, 3)).reshape(NB * BS, NB * BS)
```

```python
import jax
import jax.numpy as jnp
from jax import lax
from jax.experimental import pallas as pl
from jax.experimental.pallas import tpu as pltpu
from jax.sharding import PartitionSpec as P


AXES = ("row", "col")
NX, NY, NZ = 4, 4, 8
BS = 128
SLOTS = 32


def place(x, y, z, core):
    return (z * 2 + y % 2) * 16 + (y // 2) * 8 + x * 2 + core


def moves(dx=0, dy=0, dz=0, flip_core=0, flip_y=0):
    return [
        (
            place(x, y, z, core),
            place((x + dx) % NX, ((y + dy) % NY) ^ flip_y, (z + dz) % NZ, core ^ flip_core),
        )
        for x in range(NX)
        for y in range(NY)
        for z in range(NZ)
        for core in range(2)
    ]


TRANSPOSE = [(r * 16 + c, c * 16 + r) for r in range(16) for c in range(16)]


def shift(block, pairs):
    return lax.ppermute(block, AXES, pairs)


def scale_kernel(where_ref, obs_ref, counts_ref, inv_ref, panels_ref, out_ref, out_t_ref):
    row, col = where_ref[0], where_ref[1]
    for b in range(2):
        state = 2 * row + b
        for s in range(2):
            slot = 2 * col + s
            obs = obs_ref[state, slot]
            live = jnp.where(slot < counts_ref[state], 1.0, 0.0).astype(jnp.float32)
            weight = jnp.sqrt(inv_ref[pl.ds(obs, 1), :]) * live
            weight = jnp.broadcast_to(weight, (BS, BS)).T
            scaled = panels_ref[b, s].astype(jnp.float32) * weight
            out_ref[b, s] = scaled.astype(jnp.bfloat16)
            out_t_ref[b, s] = scaled.T.astype(jnp.bfloat16)


def scale(where, obs_of, counts, inv_var, panels):
    shape = jax.ShapeDtypeStruct((2, 2, BS, BS), jnp.bfloat16)
    smem = pl.BlockSpec(memory_space=pltpu.SMEM)
    vmem = pl.BlockSpec(memory_space=pltpu.VMEM)
    return pl.pallas_call(
        scale_kernel,
        out_shape=(shape, shape),
        in_specs=[smem, smem, smem, vmem, vmem],
        out_specs=(vmem, vmem),
        name="scale",
    )(where, obs_of, counts, inv_var, panels)


Z_STEPS = (0, -1, 1, -2, 2, -3, 3)


def product_kernel(where_ref, partner_ref, pattern_ref, *refs):
    row_refs = refs[:8]
    col_refs = refs[8:15]
    far_refs = refs[15:17]
    prior_ref, out_ref, cols_ref = refs[17:]
    row, col = where_ref[0], where_ref[1]
    z, y_low = row // 2, row % 2
    y_high, x, core = col // 8, (col // 2) % 4, col % 2
    for b in range(2):
        cols_ref[b, SLOTS] = jnp.zeros((BS, BS), jnp.bfloat16)
    for step, ref in zip(Z_STEPS, col_refs):
        source_z = (z + step + NZ) % NZ
        for sub in range(2):
            base = (source_z * 2 + (y_low if sub == 0 else 1 - y_low)) * 2
            for b in range(2):
                for s in range(2):
                    cols_ref[b, base + s] = ref[sub, b, s]
    source_z = (z + 4) % NZ
    for sub in range(2):
        base = (source_z * 2 + (y_low if sub == 0 else 1 - y_low)) * 2
        for b in range(2):
            for s in range(2):
                cols_ref[b, base + s] = far_refs[sub][b, s]
    for a in range(2):
        total = jnp.zeros((BS, 2 * BS), jnp.float32)
        for k in range(8):
            source_x = (x + (0, 3, 1, 2)[k % 4]) % NX
            source_core = core if k < 4 else 1 - core
            for sub in range(2):
                source_y = y_high if sub == 0 else 1 - y_high
                slot = (source_y * 8 + source_x * 2 + source_core) * 2
                left = jnp.concatenate([row_refs[k][sub, a, 0], row_refs[k][sub, a, 1]], axis=1)
                rows = []
                for s in range(2):
                    at = (a * SLOTS + slot + s) * 2
                    rows.append(
                        jnp.concatenate(
                            [cols_ref[b, partner_ref[at + b]] for b in range(2)], axis=1
                        )
                    )
                right = jnp.concatenate(rows, axis=0)
                total = total + jnp.dot(left, right, preferred_element_type=jnp.float32)
        for b in range(2):
            block_row, block_col = 2 * row + a, 2 * col + b
            kept = pattern_ref[jnp.minimum(block_row, block_col), jnp.maximum(block_row, block_col)] == 1
            rows, cols = slice(a * BS, (a + 1) * BS), slice(b * BS, (b + 1) * BS)
            part = total[:, cols]
            out_ref[rows, cols] = prior_ref[rows, cols] + jnp.where(kept, part, jnp.zeros_like(part))


def product(where, partner, pattern, pieces, prior):
    smem = pl.BlockSpec(memory_space=pltpu.SMEM)
    vmem = pl.BlockSpec(memory_space=pltpu.VMEM)
    return pl.pallas_call(
        product_kernel,
        out_shape=jax.ShapeDtypeStruct((2 * BS, 2 * BS), jnp.float32),
        in_specs=[smem] * 3 + [vmem] * (len(pieces) + 1),
        out_specs=vmem,
        scratch_shapes=[pltpu.VMEM((2, SLOTS + 1, BS, BS), jnp.bfloat16)],
        name="product",
    )(where, partner, pattern, *pieces, prior)


def on_device(panels, obs_of, counts, inv_var, pattern, prior):
    row = lax.axis_index("row")
    col = lax.axis_index("col")
    where = jnp.stack([row, col]).astype(jnp.int32)
    scaled, scaled_t = scale(where, obs_of, counts, inv_var, panels)
    mine = shift(scaled, TRANSPOSE)
    ring = jnp.stack([mine, shift(mine, moves(flip_y=1))])
    part = jnp.stack([scaled_t, shift(scaled_t, moves(dy=2))])
    row_pieces = [part, shift(part, moves(dx=1)), shift(part, moves(dx=-1)), shift(part, moves(dx=2))]
    row_pieces += [shift(piece, moves(flip_core=1)) for piece in row_pieces]
    up, down = [ring], [ring]
    for unused in range(3):
        up.append(shift(up[-1], moves(dz=1)))
        down.append(shift(down[-1], moves(dz=-1)))
    far = [shift(up[3][0], moves(dz=1)), shift(down[3][1], moves(dz=-1))]
    col_pieces = [ring, up[1], down[1], up[2], down[2], up[3], down[3]]

    row_ids, unused = lax.optimization_barrier((obs_of, mine))
    own = lax.dynamic_slice_in_dim(row_ids, 2 * row, 2, 0)
    other = lax.dynamic_slice_in_dim(row_ids, 2 * col, 2, 0)
    same = own[:, :, None, None] == other[None, None, :, :]
    ids = jnp.arange(SLOTS, dtype=jnp.int32)
    partner = jnp.min(jnp.where(same, ids, SLOTS), axis=3).reshape(-1)
    return product(where, partner, pattern, row_pieces + col_pieces + far, prior)


def solution(mesh):
    placed = (P("row", "col", None, None), P(), P(), P(), P(), P("row", "col"))
    return jax.shard_map(
        on_device, mesh=mesh, in_specs=placed, out_specs=P("row", "col"), check_vma=False
    )
```

```python
import jax
import jax.numpy as jnp
from jax import lax
from jax.experimental import pallas as pl
from jax.experimental.pallas import tpu as pltpu
from jax.sharding import PartitionSpec as P


AXES = ("row", "col")
NX, NY, NZ = 4, 4, 8
BS = 128
SLOTS = 32


def place(x, y, z, core):
    return (z * 2 + y % 2) * 16 + (y // 2) * 8 + x * 2 + core


def moves(dx=0, dy=0, dz=0, flip_core=0, flip_y=0):
    return [
        (
            place(x, y, z, core),
            place((x + dx) % NX, ((y + dy) % NY) ^ flip_y, (z + dz) % NZ, core ^ flip_core),
        )
        for x in range(NX)
        for y in range(NY)
        for z in range(NZ)
        for core in range(2)
    ]


TRANSPOSE = [(r * 16 + c, c * 16 + r) for r in range(16) for c in range(16)]


def shift(block, pairs):
    return lax.ppermute(block, AXES, pairs)


def scale_kernel(obs_ref, counts_ref, inv_ref, panels_ref, out_ref, out_t_ref):
    row, col = lax.axis_index("row"), lax.axis_index("col")
    for b in range(2):
        state = 2 * row + b
        for s in range(2):
            slot = 2 * col + s
            obs = obs_ref[state, slot]
            live = jnp.where(slot < counts_ref[state], 1.0, 0.0).astype(jnp.float32)
            weight = jnp.sqrt(inv_ref[pl.ds(obs, 1), :]) * live
            weight = jnp.broadcast_to(weight, (BS, BS)).T
            scaled = panels_ref[b, s].astype(jnp.float32) * weight
            out_ref[b, s] = scaled.astype(jnp.bfloat16)
            out_t_ref[b, s] = scaled.T.astype(jnp.bfloat16)


def scale(obs_of, counts, inv_var, panels):
    shape = jax.ShapeDtypeStruct((2, 2, BS, BS), jnp.bfloat16)
    smem = pl.BlockSpec(memory_space=pltpu.SMEM)
    vmem = pl.BlockSpec(memory_space=pltpu.VMEM)
    return pl.pallas_call(
        scale_kernel,
        out_shape=(shape, shape),
        in_specs=[smem, smem, vmem, vmem],
        out_specs=(vmem, vmem),
        name="scale",
    )(obs_of, counts, inv_var, panels)


Z_STEPS = (0, -1, 1, -2, 2, -3, 3)


def product_kernel(partner_ref, pattern_ref, *refs):
    row_refs = refs[:8]
    col_refs = refs[8:15]
    far_refs = refs[15:17]
    prior_ref, out_ref, cols_ref = refs[17:]
    row, col = lax.axis_index("row"), lax.axis_index("col")
    z, y_low = row // 2, row % 2
    y_high, x, core = col // 8, (col // 2) % 4, col % 2
    for b in range(2):
        cols_ref[b, SLOTS] = jnp.zeros((BS, BS), jnp.bfloat16)
    for step, ref in zip(Z_STEPS, col_refs):
        source_z = (z + step + NZ) % NZ
        for sub in range(2):
            base = (source_z * 2 + (y_low if sub == 0 else 1 - y_low)) * 2
            for b in range(2):
                for s in range(2):
                    cols_ref[b, base + s] = ref[sub, b, s]
    source_z = (z + 4) % NZ
    for sub in range(2):
        base = (source_z * 2 + (y_low if sub == 0 else 1 - y_low)) * 2
        for b in range(2):
            for s in range(2):
                cols_ref[b, base + s] = far_refs[sub][b, s]
    for a in range(2):
        total = jnp.zeros((BS, 2 * BS), jnp.float32)
        for k in range(8):
            source_x = (x + (0, 3, 1, 2)[k % 4]) % NX
            source_core = core if k < 4 else 1 - core
            for sub in range(2):
                source_y = y_high if sub == 0 else 1 - y_high
                slot = (source_y * 8 + source_x * 2 + source_core) * 2
                left = jnp.concatenate([row_refs[k][sub, a, 0], row_refs[k][sub, a, 1]], axis=1)
                rows = []
                for s in range(2):
                    at = (a * SLOTS + slot + s) * 2
                    rows.append(
                        jnp.concatenate(
                            [cols_ref[b, partner_ref[at + b]] for b in range(2)], axis=1
                        )
                    )
                right = jnp.concatenate(rows, axis=0)
                total = total + jnp.dot(left, right, preferred_element_type=jnp.float32)
        for b in range(2):
            block_row, block_col = 2 * row + a, 2 * col + b
            kept = pattern_ref[jnp.minimum(block_row, block_col), jnp.maximum(block_row, block_col)] == 1
            rows, cols = slice(a * BS, (a + 1) * BS), slice(b * BS, (b + 1) * BS)
            part = total[:, cols]
            out_ref[rows, cols] = prior_ref[rows, cols] + jnp.where(kept, part, jnp.zeros_like(part))


def product(partner, pattern, pieces, prior):
    smem = pl.BlockSpec(memory_space=pltpu.SMEM)
    vmem = pl.BlockSpec(memory_space=pltpu.VMEM)
    return pl.pallas_call(
        product_kernel,
        out_shape=jax.ShapeDtypeStruct((2 * BS, 2 * BS), jnp.float32),
        in_specs=[smem] * 2 + [vmem] * (len(pieces) + 1),
        out_specs=vmem,
        scratch_shapes=[pltpu.VMEM((2, SLOTS + 1, BS, BS), jnp.bfloat16)],
        name="product",
    )(partner, pattern, *pieces, prior)


def partner_slots(obs_of, row, col):
    own = lax.dynamic_slice_in_dim(obs_of, 2 * row, 2, 0)
    other = lax.dynamic_slice_in_dim(obs_of, 2 * col, 2, 0)
    same = own[:, :, None, None] == other[None, None, :, :]
    ids = jnp.arange(SLOTS, dtype=jnp.int32)
    return jnp.min(jnp.where(same, ids, SLOTS), axis=3).reshape(-1)


def on_device(panels, obs_of, counts, inv_var, pattern, prior):
    row = lax.axis_index("row")
    col = lax.axis_index("col")
    scaled, scaled_t = scale(obs_of, counts, inv_var, panels)
    mine = shift(scaled, TRANSPOSE)
    later_obs, scaled_t = lax.optimization_barrier((obs_of, scaled_t))
    partner = partner_slots(later_obs, row, col)
    part = jnp.stack([scaled_t, shift(scaled_t, moves(dy=2))])
    row_pieces = [part, shift(part, moves(dx=1)), shift(part, moves(dx=-1)), shift(part, moves(dx=2))]
    mine, partner, *row_pieces = lax.optimization_barrier((mine, partner, *row_pieces))
    ring = jnp.stack([mine, shift(mine, moves(flip_y=1))])
    other_core = [shift(piece, moves(flip_core=1)) for piece in row_pieces]
    up, down = [ring], [ring]
    for step in range(3):
        ahead = shift(up[-1], moves(dz=1))
        behind = shift(down[-1], moves(dz=-1))
        if step == 0:
            ahead, behind, *other_core = lax.optimization_barrier((ahead, behind, *other_core))
        up.append(ahead)
        down.append(behind)
    far = [shift(up[3][0], moves(dz=1)), shift(down[3][1], moves(dz=-1))]
    col_pieces = [ring, up[1], down[1], up[2], down[2], up[3], down[3]]
    return product(partner, pattern, row_pieces + other_core + col_pieces + far, prior)


def solution(mesh):
    placed = (P("row", "col", None, None), P(), P(), P(), P(), P("row", "col"))
    return jax.shard_map(
        on_device, mesh=mesh, in_specs=placed, out_specs=P("row", "col"), check_vma=False
    )
```

```python
import jax
import jax.numpy as jnp
from jax import lax
from jax.experimental import pallas as pl
from jax.experimental.pallas import tpu as pltpu
from jax.sharding import PartitionSpec as P


AXES = ("row", "col")
NX, NY, NZ = 4, 4, 8
BS = 128
SLOTS = 32
NOBS = 64


def place(x, y, z, core):
    return (z * 2 + y % 2) * 16 + (y // 2) * 8 + x * 2 + core


def moves(dx=0, dy=0, dz=0, flip_core=0, flip_y=0):
    return [
        (
            place(x, y, z, core),
            place((x + dx) % NX, ((y + dy) % NY) ^ flip_y, (z + dz) % NZ, core ^ flip_core),
        )
        for x in range(NX)
        for y in range(NY)
        for z in range(NZ)
        for core in range(2)
    ]


Z_OFFSETS = {(0, 0): 4, (1, 0): 3, (3, 0): -3, (2, 0): 2, (0, 1): -2, (1, 1): 1, (3, 1): -1, (2, 1): 0}
DISPLACED = {offset % NZ: shift for shift, offset in Z_OFFSETS.items()}


def spread():
    pairs = []
    for row in range(16):
        z = row // 2
        for col in range(16):
            y_high, x, core = col // 8, (col // 2) % 4, col % 2
            offset = Z_OFFSETS[((z % 4 - x) % 4, (z // 4) ^ y_high)]
            pairs.append((row * 16 + col, ((z + offset) % NZ * 2 + core) * 16 + row))
    return pairs


SPREAD = spread()
Z_STEPS = (0, -1, 1, -2, 2, -3, 3, -4)


def shift(block, pairs):
    return lax.ppermute(block, AXES, pairs)


def scale_kernel(obs_ref, counts_ref, inv_ref, panels_ref, out_ref):
    row, col = lax.axis_index("row"), lax.axis_index("col")
    for b in range(2):
        state = 2 * row + b
        for s in range(2):
            slot = 2 * col + s
            obs = obs_ref[state, slot]
            live = jnp.where(slot < counts_ref[state], 1.0, 0.0).astype(jnp.float32)
            weight = jnp.sqrt(inv_ref[pl.ds(obs, 1), :]) * live
            weight = jnp.broadcast_to(weight, (BS, BS)).T
            scaled = panels_ref[b, s].astype(jnp.float32) * weight
            out_ref[b, s] = scaled.astype(jnp.bfloat16)


SMEM = pl.BlockSpec(memory_space=pltpu.SMEM)
VMEM = pl.BlockSpec(memory_space=pltpu.VMEM)
ANY = pl.BlockSpec(memory_space=pl.ANY)


def scale(obs_of, counts, inv_var, panels):
    return pl.pallas_call(
        scale_kernel,
        out_shape=jax.ShapeDtypeStruct((2, 2, BS, BS), jnp.bfloat16),
        in_specs=[SMEM, SMEM, VMEM, VMEM],
        out_specs=VMEM,
        name="scale",
    )(obs_of, counts, inv_var, panels)


def turn_kernel(obs_ref, scaled_ref, out_ref, partner_ref, slot_ref):
    row, col = lax.axis_index("row"), lax.axis_index("col")
    for b in range(2):
        for s in range(2):
            out_ref[b, s] = scaled_ref[b, s].T

    def clear(k, unused):
        slot_ref[k] = SLOTS
        return unused

    def enter(q, unused):
        for b in range(2):
            slot_ref[b * NOBS + obs_ref[2 * col + b, q]] = q
        return unused

    def find(p, unused):
        for a in range(2):
            obs = obs_ref[2 * row + a, p]
            for b in range(2):
                partner_ref[(a * SLOTS + p) * 2 + b] = slot_ref[b * NOBS + obs]
        return unused

    lax.fori_loop(0, 2 * NOBS, clear, 0, unroll=8)
    lax.fori_loop(0, SLOTS, enter, 0, unroll=4)
    lax.fori_loop(0, SLOTS, find, 0, unroll=4)


def turn(obs_of, scaled):
    return pl.pallas_call(
        turn_kernel,
        out_shape=(
            jax.ShapeDtypeStruct((2, 2, BS, BS), jnp.bfloat16),
            jax.ShapeDtypeStruct((4 * SLOTS,), jnp.int32),
        ),
        in_specs=[SMEM, VMEM],
        out_specs=(VMEM, SMEM),
        scratch_shapes=[pltpu.SMEM((2 * NOBS,), jnp.int32)],
        name="turn",
    )(obs_of, scaled)


def displaced(offset):
    steps, half = jnp.int32(0), jnp.int32(0)
    for at, (dx, dy) in DISPLACED.items():
        steps = jnp.where(offset == at, dx, steps)
        half = jnp.where(offset == at, dy, half)
    return steps, half


def product_kernel(partner_ref, pattern_ref, *refs):
    row_refs, col_refs = refs[:8], refs[8:24]
    prior_ref, out_ref, rows_ref, cols_ref, held_ref, row_sem, col_sem, prior_sem = refs[24:]
    row, col = lax.axis_index("row"), lax.axis_index("col")
    y_low = row % 2
    y_high, x, core = col // 8, (col // 2) % 4, col % 2
    col_copies = []
    for k, step in enumerate(Z_STEPS):
        steps, half = displaced((row // 2 + step - col // 2 + 2 * NZ) % NZ)
        source = (y_high + half) % 2 * 8 + (x - steps + NX) % NX * 2
        for sub in range(2):
            slot = 2 * (source + (y_low if sub == 0 else 1 - y_low))
            for b in range(2):
                col_copies.append(
                    pltpu.make_async_copy(
                        col_refs[2 * k + sub].at[b],
                        cols_ref.at[b, pl.ds(slot, 2)],
                        col_sem.at[2 * k + sub, b],
                    )
                )
    row_copies = [
        pltpu.make_async_copy(row_refs[k], rows_ref.at[k], row_sem.at[k]) for k in range(8)
    ]
    prior_copy = pltpu.make_async_copy(prior_ref, held_ref, prior_sem)
    for copy in col_copies:
        copy.start()
    for copy in row_copies:
        copy.start()
    prior_copy.start()
    for b in range(2):
        cols_ref[b, SLOTS] = jnp.zeros((BS, BS), jnp.bfloat16)
    for copy in col_copies:
        copy.wait()
    for a in range(2):
        total = jnp.zeros((BS, 2 * BS), jnp.float32)
        for k in range(8):
            if a == 0:
                row_copies[k].wait()
            source_x = (x + (0, 3, 1, 2)[k % 4]) % NX
            source_core = core if k < 4 else 1 - core
            for sub in range(2):
                source_y = y_high if sub == 0 else 1 - y_high
                slot = (source_y * 8 + source_x * 2 + source_core) * 2
                left = jnp.concatenate([rows_ref[k, sub, a, 0], rows_ref[k, sub, a, 1]], axis=1)
                rights = []
                for s in range(2):
                    at = (a * SLOTS + slot + s) * 2
                    rights.append(
                        jnp.concatenate(
                            [cols_ref[b, partner_ref[at + b]] for b in range(2)], axis=1
                        )
                    )
                right = jnp.concatenate(rights, axis=0)
                total = total + jnp.dot(left, right, preferred_element_type=jnp.float32)
        if a == 0:
            prior_copy.wait()
        for b in range(2):
            block_row, block_col = 2 * row + a, 2 * col + b
            low, high = jnp.minimum(block_row, block_col), jnp.maximum(block_row, block_col)
            kept = pattern_ref[low, high] == 1
            rows, cols = slice(a * BS, (a + 1) * BS), slice(b * BS, (b + 1) * BS)
            part = total[:, cols]
            out_ref[rows, cols] = held_ref[rows, cols] + jnp.where(kept, part, jnp.zeros_like(part))


def product(partner, pattern, pieces, prior):
    return pl.pallas_call(
        product_kernel,
        out_shape=jax.ShapeDtypeStruct((2 * BS, 2 * BS), jnp.float32),
        in_specs=[SMEM, SMEM] + [ANY] * (len(pieces) + 1),
        out_specs=VMEM,
        scratch_shapes=[
            pltpu.VMEM((8, 2, 2, 2, BS, BS), jnp.bfloat16),
            pltpu.VMEM((2, SLOTS + 1, BS, BS), jnp.bfloat16),
            pltpu.VMEM((2 * BS, 2 * BS), jnp.float32),
            pltpu.SemaphoreType.DMA((8,)),
            pltpu.SemaphoreType.DMA((16, 2)),
            pltpu.SemaphoreType.DMA,
        ],
        compiler_params=pltpu.CompilerParams(vmem_limit_bytes=12 * 2**20),
        name="product",
    )(partner, pattern, *pieces, prior)


def on_device(panels, obs_of, counts, inv_var, pattern, prior):
    scaled = scale(obs_of, counts, inv_var, panels)
    mine = shift(scaled, SPREAD)
    scaled_t, partner = turn(obs_of, scaled)
    part = jnp.stack([scaled_t, shift(scaled_t, moves(dy=2))])
    row_pieces = [
        part, shift(part, moves(dx=1)), shift(part, moves(dx=-1)), shift(part, moves(dx=2))
    ]
    row_pieces += [shift(piece, moves(flip_core=1)) for piece in row_pieces]
    up, down = [mine], [mine]
    for step in range(1, 5):
        up.append(shift(up[-1], moves(dz=1)))
        if step < 4:
            down.append(shift(down[-1], moves(dz=-1)))
    swapped = shift(mine, moves(flip_y=1))
    col_pieces = [mine, swapped]
    for step in range(1, 4):
        for piece in (up[step], down[step]):
            col_pieces += [piece, shift(piece, moves(flip_y=1))]
    col_pieces += [up[4], shift(swapped, moves(dz=4))]
    return product(partner, pattern, row_pieces + col_pieces, prior)


def solution(mesh):
    placed = (P("row", "col", None, None), P(), P(), P(), P(), P("row", "col"))
    return jax.shard_map(
        on_device, mesh=mesh, in_specs=placed, out_specs=P("row", "col"), check_vma=False
    )
```

```python
import functools

import jax
import jax.numpy as jnp
from jax import lax
from jax.experimental import pallas as pl
from jax.experimental.pallas import tpu as pltpu
from jax.sharding import PartitionSpec as P


AXES = ("row", "col")
NX, NY, NZ = 4, 4, 8
BS = 128
SLOTS = 32
NOBS = 64


def place(x, y, z, core):
    return (z * 2 + y % 2) * 16 + (y // 2) * 8 + x * 2 + core


def moves(dx=0, dy=0, dz=0, flip_core=0, flip_y=0):
    return [
        (
            place(x, y, z, core),
            place((x + dx) % NX, ((y + dy) % NY) ^ flip_y, (z + dz) % NZ, core ^ flip_core),
        )
        for x in range(NX)
        for y in range(NY)
        for z in range(NZ)
        for core in range(2)
    ]


Z_OFFSETS = {(0, 0): 4, (1, 0): 3, (3, 0): -3, (2, 0): 2, (0, 1): -2, (1, 1): 1, (3, 1): -1, (2, 1): 0}
DISPLACED = {offset % NZ: shift for shift, offset in Z_OFFSETS.items()}


def spread():
    pairs = []
    for row in range(16):
        z = row // 2
        for col in range(16):
            y_high, x, core = col // 8, (col // 2) % 4, col % 2
            offset = Z_OFFSETS[((z % 4 - x) % 4, (z // 4) ^ y_high)]
            pairs.append((row * 16 + col, ((z + offset) % NZ * 2 + core) * 16 + row))
    return pairs


SPREAD = spread()
UP, DOWN = moves(dz=1), moves(dz=-1)
RING = [pair for pair in UP if pair[0] % 2 == 0] + [pair for pair in DOWN if pair[0] % 2 == 1]
PIECES = [(0, 0), (0, 1)] + [(sign * t, sub) for t in (1, 2, 3) for sub in (0, 1) for sign in (-1, 1)] + [(4, 0), (4, 1)]


def shift(block, pairs):
    return lax.ppermute(block, AXES, pairs)


def scale_kernel(obs_ref, counts_ref, inv_ref, panels_ref, out_ref):
    row, col = lax.axis_index("row"), lax.axis_index("col")
    for b in range(2):
        state = 2 * row + b
        for s in range(2):
            slot = 2 * col + s
            obs = obs_ref[state, slot]
            live = jnp.where(slot < counts_ref[state], 1.0, 0.0).astype(jnp.float32)
            weight = jnp.sqrt(inv_ref[pl.ds(obs, 1), :]) * live
            weight = jnp.broadcast_to(weight, (BS, BS)).T
            scaled = panels_ref[b, s].astype(jnp.float32) * weight
            out_ref[b, s] = scaled.astype(jnp.bfloat16)


SMEM = pl.BlockSpec(memory_space=pltpu.SMEM)
VMEM = pl.BlockSpec(memory_space=pltpu.VMEM)
ANY = pl.BlockSpec(memory_space=pl.ANY)


def scale(obs_of, counts, inv_var, panels):
    return pl.pallas_call(
        scale_kernel,
        out_shape=jax.ShapeDtypeStruct((2, 2, BS, BS), jnp.bfloat16),
        in_specs=[SMEM, SMEM, VMEM, VMEM],
        out_specs=VMEM,
        name="scale",
    )(obs_of, counts, inv_var, panels)


def turn_kernel(obs_ref, scaled_ref, out_ref, partner_ref, slot_ref):
    row, col = lax.axis_index("row"), lax.axis_index("col")
    for b in range(2):
        for s in range(2):
            out_ref[b, s] = scaled_ref[b, s].T

    def clear(k, unused):
        slot_ref[k] = SLOTS
        return unused

    def enter(q, unused):
        for b in range(2):
            slot_ref[b * NOBS + obs_ref[2 * col + b, q]] = q
        return unused

    def find(p, unused):
        for a in range(2):
            obs = obs_ref[2 * row + a, p]
            for b in range(2):
                partner_ref[(a * SLOTS + p) * 2 + b] = slot_ref[b * NOBS + obs]
        return unused

    lax.fori_loop(0, 2 * NOBS, clear, 0, unroll=8)
    lax.fori_loop(0, SLOTS, enter, 0, unroll=4)
    lax.fori_loop(0, SLOTS, find, 0, unroll=4)


def turn(obs_of, scaled):
    return pl.pallas_call(
        turn_kernel,
        out_shape=(
            jax.ShapeDtypeStruct((2, 2, BS, BS), jnp.bfloat16),
            jax.ShapeDtypeStruct((4 * SLOTS,), jnp.int32),
        ),
        in_specs=[SMEM, VMEM],
        out_specs=(VMEM, SMEM),
        scratch_shapes=[pltpu.SMEM((2 * NOBS,), jnp.int32)],
        name="turn",
    )(obs_of, scaled)


def join_kernel(by_core, first_ref, second_ref, out_ref):
    at = lax.axis_index("col") % 2 if by_core else 0
    out_ref[at] = first_ref[...]
    out_ref[1 - at] = second_ref[...]


def join(first, second, by_core=False):
    return pl.pallas_call(
        functools.partial(join_kernel, by_core),
        out_shape=jax.ShapeDtypeStruct((2, *first.shape), first.dtype),
        in_specs=[VMEM, VMEM],
        out_specs=VMEM,
        compiler_params=pltpu.CompilerParams(vmem_limit_bytes=2 * 2**20),
        name="join",
    )(first, second)


def displaced(offset):
    steps, half = jnp.int32(0), jnp.int32(0)
    for at, (dx, dy) in DISPLACED.items():
        steps = jnp.where(offset == at, dx, steps)
        half = jnp.where(offset == at, dy, half)
    return steps, half


def product_kernel(partner_ref, pattern_ref, *refs):
    row_refs, col_refs = refs[:8], refs[8:24]
    prior_ref, out_ref, cols_ref = refs[24:]
    row, col = lax.axis_index("row"), lax.axis_index("col")
    y_low = row % 2
    y_high, x, core = col // 8, (col // 2) % 4, col % 2
    for b in range(2):
        cols_ref[b, SLOTS] = jnp.zeros((BS, BS), jnp.bfloat16)
    way = 1 - 2 * core
    for ref, (step, sub) in zip(col_refs, PIECES):
        steps, half = displaced((row // 2 + step * way - col // 2 + 2 * NZ) % NZ)
        source = (y_high + half) % 2 * 8 + (x - steps + NX) % NX * 2
        slot = 2 * (source + (y_low if sub == 0 else 1 - y_low))
        for b in range(2):
            for s in range(2):
                cols_ref[b, slot + s] = ref[core, b, s] if len(ref.shape) == 5 else ref[b, s]
    for a in range(2):
        total = jnp.zeros((BS, 2 * BS), jnp.float32)
        for k in range(8):
            source_x = (x + (0, 3, 1, 2)[k % 4]) % NX
            source_core = core if k < 4 else 1 - core
            for sub in range(2):
                source_y = y_high if sub == 0 else 1 - y_high
                slot = (source_y * 8 + source_x * 2 + source_core) * 2
                left = jnp.concatenate([row_refs[k][sub, a, 0], row_refs[k][sub, a, 1]], axis=1)
                rights = []
                for s in range(2):
                    at = (a * SLOTS + slot + s) * 2
                    rights.append(
                        jnp.concatenate(
                            [cols_ref[b, partner_ref[at + b]] for b in range(2)], axis=1
                        )
                    )
                right = jnp.concatenate(rights, axis=0)
                total = total + jnp.dot(left, right, preferred_element_type=jnp.float32)
        for b in range(2):
            block_row, block_col = 2 * row + a, 2 * col + b
            low, high = jnp.minimum(block_row, block_col), jnp.maximum(block_row, block_col)
            kept = pattern_ref[low, high] == 1
            rows, cols = slice(a * BS, (a + 1) * BS), slice(b * BS, (b + 1) * BS)
            part = total[:, cols]
            out_ref[rows, cols] = prior_ref[rows, cols] + jnp.where(kept, part, jnp.zeros_like(part))


def product(partner, pattern, pieces, prior):
    return pl.pallas_call(
        product_kernel,
        out_shape=jax.ShapeDtypeStruct((2 * BS, 2 * BS), jnp.float32),
        in_specs=[SMEM, SMEM] + [VMEM] * (len(pieces) + 1),
        out_specs=VMEM,
        scratch_shapes=[pltpu.VMEM((2, SLOTS + 1, BS, BS), jnp.bfloat16)],
        compiler_params=pltpu.CompilerParams(vmem_limit_bytes=12 * 2**20),
        name="product",
    )(partner, pattern, *pieces, prior)


def on_device(panels, obs_of, counts, inv_var, pattern, prior):
    scaled = scale(obs_of, counts, inv_var, panels)
    mine = shift(scaled, SPREAD)
    scaled_t, partner = turn(obs_of, scaled)
    part = join(scaled_t, shift(scaled_t, moves(dy=2)))
    row_pieces = [part, shift(part, moves(dx=1)), shift(part, moves(dx=-1)), shift(part, moves(dx=2))]
    row_pieces += [shift(piece, OTHER_CORE) for piece in row_pieces]
    ring = join(mine, shift(mine, OTHER_CORE), by_core=True)
    swapped = shift(mine, OTHER_Y)
    col_pieces = [mine, swapped]
    for _ in range(1, 4):
        ring = shift(ring, RING)
        turned = shift(ring, OTHER_Y)
        col_pieces += [ring, shift(ring, OTHER_CORE)]
        col_pieces += [turned, shift(turned, OTHER_CORE)]
    col_pieces += [shift(ring, RING), shift(swapped, moves(dz=4))]
    return product(partner, pattern, row_pieces + col_pieces, prior)


OTHER_CORE, OTHER_Y = moves(flip_core=1), moves(flip_y=1)


def solution(mesh):
    placed = (P("row", "col", None, None), P(), P(), P(), P(), P("row", "col"))
    return jax.shard_map(
        on_device, mesh=mesh, in_specs=placed, out_specs=P("row", "col"), check_vma=False
    )
```

```python
import functools

import jax
import jax.numpy as jnp
from jax import lax
from jax.experimental import pallas as pl
from jax.experimental.pallas import tpu as pltpu
from jax.sharding import PartitionSpec as P


AXES = ("row", "col")
NX, NY, NZ = 4, 4, 8
BS = 128
SLOTS = 32
NOBS = 64


def place(x, y, z, core):
    return (z * 2 + y % 2) * 16 + (y // 2) * 8 + x * 2 + core


def moves(dx=0, dy=0, dz=0, flip_core=0, flip_y=0):
    return [
        (
            place(x, y, z, core),
            place((x + dx) % NX, ((y + dy) % NY) ^ flip_y, (z + dz) % NZ, core ^ flip_core),
        )
        for x in range(NX)
        for y in range(NY)
        for z in range(NZ)
        for core in range(2)
    ]


Z_OFFSETS = {(0, 0): 4, (1, 0): 3, (3, 0): -3, (2, 0): 2, (0, 1): -2, (1, 1): 1, (3, 1): -1, (2, 1): 0}
DISPLACED = {offset % NZ: shift for shift, offset in Z_OFFSETS.items()}


def spread(flip):
    pairs = []
    for row in range(16):
        z = row // 2
        for col in range(16):
            y_high, x, core = col // 8, (col // 2) % 4, col % 2
            offset = Z_OFFSETS[((z % 4 - x) % 4, (z // 4) ^ y_high)]
            half = core ^ flip
            pairs.append((row * 16 + col, ((z + offset) % NZ * 2 + half) * 16 + row))
    return pairs


SPREAD = spread(0), spread(1)
UP, DOWN = moves(dz=1), moves(dz=-1)
RING = [pair for pair in UP if pair[0] % 2 == 0] + [pair for pair in DOWN if pair[0] % 2 == 1]
PIECES = (0, -1, 1, -2, 2, -3, 3, 4)
HALF = BS // 2


def shift(block, pairs):
    return lax.ppermute(block, AXES, pairs)


def scale_kernel(obs_ref, counts_ref, inv_ref, panels_ref, out_ref, same_ref, cross_ref):
    row, col = lax.axis_index("row"), lax.axis_index("col")
    core = col % 2
    for b in range(2):
        state = 2 * row + b
        for s in range(2):
            slot = 2 * col + s
            obs = obs_ref[state, slot]
            live = jnp.where(slot < counts_ref[state], 1.0, 0.0).astype(jnp.float32)
            weight = jnp.sqrt(inv_ref[pl.ds(obs, 1), :]) * live
            weight = jnp.broadcast_to(weight, (BS, BS)).T
            scaled = panels_ref[b, s].astype(jnp.float32) * weight
            out_ref[b, s] = scaled.astype(jnp.bfloat16)
            same_ref[b, s] = out_ref[b, s, pl.ds(pl.multiple_of(core * HALF, HALF), HALF), :]
            cross_ref[b, s] = out_ref[b, s, pl.ds(pl.multiple_of((1 - core) * HALF, HALF), HALF), :]


SMEM = pl.BlockSpec(memory_space=pltpu.SMEM)
VMEM = pl.BlockSpec(memory_space=pltpu.VMEM)


def scale(obs_of, counts, inv_var, panels):
    half = jax.ShapeDtypeStruct((2, 2, HALF, BS), jnp.bfloat16)
    return pl.pallas_call(
        scale_kernel,
        out_shape=(jax.ShapeDtypeStruct((2, 2, BS, BS), jnp.bfloat16), half, half),
        in_specs=[SMEM, SMEM, VMEM, VMEM],
        out_specs=(VMEM, VMEM, VMEM),
        name="scale",
    )(obs_of, counts, inv_var, panels)


def turn_kernel(obs_ref, scaled_ref, keep_ref, give_ref, partner_ref, slot_ref):
    row, col = lax.axis_index("row"), lax.axis_index("col")
    y_low = row % 2
    for ref, half in ((keep_ref, y_low), (give_ref, 1 - y_low)):
        start = pl.multiple_of(half * HALF, HALF)
        for b in range(2):
            both = [scaled_ref[b, s, pl.ds(start, HALF), :] for s in range(2)]
            ref[b] = jnp.concatenate(both, axis=0).T

    def clear(k, unused):
        slot_ref[k] = SLOTS
        return unused

    def enter(q, unused):
        for b in range(2):
            slot_ref[b * NOBS + obs_ref[2 * col + b, q]] = q
        return unused

    def find(p, unused):
        for a in range(4):
            obs = obs_ref[row // 2 * 4 + a, p]
            for b in range(2):
                partner_ref[(a * SLOTS + p) * 2 + b] = slot_ref[b * NOBS + obs]
        return unused

    lax.fori_loop(0, 2 * NOBS, clear, 0, unroll=8)
    lax.fori_loop(0, SLOTS, enter, 0, unroll=4)
    lax.fori_loop(0, SLOTS, find, 0, unroll=4)


def turn(obs_of, scaled):
    turned = jax.ShapeDtypeStruct((2, BS, BS), jnp.bfloat16)
    return pl.pallas_call(
        turn_kernel,
        out_shape=(turned, turned, jax.ShapeDtypeStruct((8 * SLOTS,), jnp.int32)),
        in_specs=[SMEM, VMEM],
        out_specs=(VMEM, VMEM, SMEM),
        scratch_shapes=[pltpu.SMEM((2 * NOBS,), jnp.int32)],
        name="turn",
    )(obs_of, scaled)


def join_kernel(order, first_ref, second_ref, out_ref):
    at = 0
    if order == "core":
        at = lax.axis_index("col") % 2
    elif order == "y_low":
        at = lax.axis_index("row") % 2
    out_ref[at] = first_ref[...]
    out_ref[1 - at] = second_ref[...]


def join(first, second, order=None):
    return pl.pallas_call(
        functools.partial(join_kernel, order),
        out_shape=jax.ShapeDtypeStruct((2, *first.shape), first.dtype),
        in_specs=[VMEM, VMEM],
        out_specs=VMEM,
        compiler_params=pltpu.CompilerParams(vmem_limit_bytes=2 * 2**20),
        name="join",
    )(first, second)


def displaced(offset):
    steps, half = jnp.int32(0), jnp.int32(0)
    for at, (dx, dy) in DISPLACED.items():
        steps = jnp.where(offset == at, dx, steps)
        half = jnp.where(offset == at, dy, half)
    return steps, half


def multiply(group, partner_ref, row_refs, cols_ref, out_ref):
    col = lax.axis_index("col")
    y_high, x, core = col // 8, (col // 2) % 4, col % 2
    for a in range(2):
        total = jnp.zeros((BS, 2 * BS), jnp.float32)
        for k in range(8):
            source_x = (x + (0, 3, 1, 2)[k % 4]) % NX
            source_core = core if k < 4 else 1 - core
            lefts, rights = [], []
            for sub in range(2):
                source_y = y_high if sub == 0 else 1 - y_high
                slot = (source_y * 8 + source_x * 2 + source_core) * 2
                lefts.append(row_refs[k][sub, group, a])
                for s in range(2):
                    at = ((group * 2 + a) * SLOTS + slot + s) * 2
                    blocks = [cols_ref[b, partner_ref[at + b]] for b in range(2)]
                    rights.append(jnp.concatenate(blocks, axis=1))
            left, right = jnp.concatenate(lefts, axis=1), jnp.concatenate(rights, axis=0)
            total = total + jnp.dot(left, right, preferred_element_type=jnp.float32)
        out_ref[a * BS : (a + 1) * BS, :] = total


def give_kernel(partner_ref, *refs):
    row_refs, col_refs = refs[:8], refs[8:16]
    out_ref, cols_ref = refs[16:]
    row, col = lax.axis_index("row"), lax.axis_index("col")
    z, y_low = row // 2, row % 2
    y_high, x, core = col // 8, (col // 2) % 4, col % 2
    for b in range(2):
        cols_ref[b, SLOTS] = jnp.zeros((HALF, BS), jnp.bfloat16)
    way = 1 - 2 * core
    for ref, step in zip(col_refs, PIECES):
        steps, half = displaced((z + step * way - col // 2 + 2 * NZ) % NZ)
        source = (y_high + half) % 2 * 8 + (x - steps + NX) % NX * 2
        for cross in range(2):
            slot = 2 * (source + (y_low if cross == 0 else 1 - y_low))
            for b in range(2):
                for s in range(2):
                    cols_ref[b, slot + s] = ref[core, cross, b, s]
    multiply(1 - y_low, partner_ref, row_refs, cols_ref, out_ref)


def keep_kernel(partner_ref, *refs):
    row_refs = refs[:8]
    cols_ref, out_ref = refs[8:]
    multiply(lax.axis_index("row") % 2, partner_ref, row_refs, cols_ref, out_ref)


def finish_kernel(pattern_ref, keep_ref, taken_ref, prior_ref, out_ref):
    row, col = lax.axis_index("row"), lax.axis_index("col")
    for a in range(2):
        for b in range(2):
            block_row, block_col = 2 * row + a, 2 * col + b
            low, high = jnp.minimum(block_row, block_col), jnp.maximum(block_row, block_col)
            kept = pattern_ref[low, high] == 1
            at = slice(a * BS, (a + 1) * BS), slice(b * BS, (b + 1) * BS)
            part = keep_ref[at] + taken_ref[at]
            out_ref[at] = prior_ref[at] + jnp.where(kept, part, jnp.zeros_like(part))


TILE = jax.ShapeDtypeStruct((2 * BS, 2 * BS), jnp.float32)
COLS = jax.ShapeDtypeStruct((2, SLOTS + 1, HALF, BS), jnp.bfloat16)


def local(kernel, out_shape, smalls, arrays):
    many = isinstance(out_shape, tuple)
    return pl.pallas_call(
        kernel,
        out_shape=out_shape,
        in_specs=[SMEM] * len(smalls) + [VMEM] * len(arrays),
        out_specs=(VMEM,) * len(out_shape) if many else VMEM,
        compiler_params=pltpu.CompilerParams(vmem_limit_bytes=12 * 2**20),
    )(*smalls, *arrays)


def on_device(panels, obs_of, counts, inv_var, pattern, prior):
    scaled, same, cross = scale(obs_of, counts, inv_var, panels)
    mine = shift(same, SPREAD[0]), shift(cross, SPREAD[1])
    keep_t, give_t, partner = turn(obs_of, scaled)
    part = join(keep_t, shift(give_t, OTHER_Y), "y_low")
    part = join(part, shift(part, moves(dy=2)))
    row_pieces = [
        part, shift(part, moves(dx=1)), shift(part, moves(dx=-1)), shift(part, moves(dx=2))
    ]
    row_pieces += [shift(piece, OTHER_CORE) for piece in row_pieces]
    own = join(*mine)
    ring = join(own, shift(own, OTHER_CORE), "core")
    col_pieces = [ring]
    for _ in range(1, 4):
        ring = shift(ring, RING)
        col_pieces += [ring, shift(ring, OTHER_CORE)]
    col_pieces.append(shift(ring, RING))
    give, cols = local(give_kernel, (TILE, COLS), [partner], row_pieces + col_pieces)
    taken = shift(give, OTHER_Y)
    keep = local(keep_kernel, TILE, [partner], row_pieces + [cols])
    return local(finish_kernel, TILE, [pattern], [keep, taken, prior])


OTHER_CORE, OTHER_Y = moves(flip_core=1), moves(flip_y=1)


def solution(mesh):
    placed = (P("row", "col", None, None), P(), P(), P(), P(), P("row", "col"))
    return jax.shard_map(
        on_device, mesh=mesh, in_specs=placed, out_specs=P("row", "col"), check_vma=False
    )
```

```python
import functools

import jax
import jax.numpy as jnp
from jax import lax
from jax.experimental import pallas as pl
from jax.experimental.pallas import tpu as pltpu
from jax.sharding import PartitionSpec as P


AXES = ("row", "col")
NX, NY, NZ = 4, 4, 8
BS = 128
SLOTS = 32
NOBS = 64


def place(x, y, z, core):
    return (z * 2 + y % 2) * 16 + (y // 2) * 8 + x * 2 + core


def moves(dx=0, dy=0, dz=0, flip_core=0, flip_y=0):
    return [
        (
            place(x, y, z, core),
            place((x + dx) % NX, ((y + dy) % NY) ^ flip_y, (z + dz) % NZ, core ^ flip_core),
        )
        for x in range(NX)
        for y in range(NY)
        for z in range(NZ)
        for core in range(2)
    ]


Z_OFFSETS = {(0, 0): 4, (1, 0): 3, (3, 0): -3, (2, 0): 2, (0, 1): -2, (1, 1): 1, (3, 1): -1, (2, 1): 0}
DISPLACED = {offset % NZ: shift for shift, offset in Z_OFFSETS.items()}


def spread(flip):
    pairs = []
    for row in range(16):
        z = row // 2
        for col in range(16):
            y_high, x, core = col // 8, (col // 2) % 4, col % 2
            offset = Z_OFFSETS[((z % 4 - x) % 4, (z // 4) ^ y_high)]
            half = core ^ flip
            pairs.append((row * 16 + col, ((z + offset) % NZ * 2 + half) * 16 + row))
    return pairs


SPREAD = spread(0), spread(1)
UP, DOWN = moves(dz=1), moves(dz=-1)
RING = [pair for pair in UP if pair[0] % 2 == 0] + [pair for pair in DOWN if pair[0] % 2 == 1]
PIECES = (0, -1, 1, -2, 2, -3, 3, 4)
HALF = BS // 2


def shift(block, pairs):
    return lax.ppermute(block, AXES, pairs)


def scale_kernel(obs_ref, counts_ref, inv_ref, panels_ref, out_ref, same_ref, cross_ref):
    row, col = lax.axis_index("row"), lax.axis_index("col")
    core = col % 2
    for b in range(2):
        state = 2 * row + b
        for s in range(2):
            slot = 2 * col + s
            obs = obs_ref[state, slot]
            live = jnp.where(slot < counts_ref[state], 1.0, 0.0).astype(jnp.float32)
            weight = jnp.sqrt(inv_ref[pl.ds(obs, 1), :]) * live
            weight = jnp.broadcast_to(weight, (BS, BS)).T
            scaled = panels_ref[b, s].astype(jnp.float32) * weight
            out_ref[b, s] = scaled.astype(jnp.bfloat16)
            same_ref[b, s] = out_ref[b, s, pl.ds(pl.multiple_of(core * HALF, HALF), HALF), :]
            cross_ref[b, s] = out_ref[b, s, pl.ds(pl.multiple_of((1 - core) * HALF, HALF), HALF), :]


SMEM = pl.BlockSpec(memory_space=pltpu.SMEM)
VMEM = pl.BlockSpec(memory_space=pltpu.VMEM)
SMALL = pltpu.CompilerParams(vmem_limit_bytes=2 * 2**20)


def scale(obs_of, counts, inv_var, panels):
    half = jax.ShapeDtypeStruct((2, 2, HALF, BS), jnp.bfloat16)
    return pl.pallas_call(
        scale_kernel,
        out_shape=(jax.ShapeDtypeStruct((2, 2, BS, BS), jnp.bfloat16), half, half),
        in_specs=[SMEM, SMEM, VMEM, VMEM],
        out_specs=(VMEM, VMEM, VMEM),
        name="scale",
    )(obs_of, counts, inv_var, panels)


def turn_kernel(scaled_ref, keep_ref, give_ref):
    y_low = lax.axis_index("row") % 2
    for ref, half in ((keep_ref, y_low), (give_ref, 1 - y_low)):
        start = pl.multiple_of(half * HALF, HALF)
        for b in range(2):
            both = [scaled_ref[b, s, pl.ds(start, HALF), :] for s in range(2)]
            ref[b] = jnp.concatenate(both, axis=0).T


def turn(scaled):
    turned = jax.ShapeDtypeStruct((2, BS, BS), jnp.bfloat16)
    return pl.pallas_call(
        turn_kernel,
        out_shape=(turned, turned),
        in_specs=[VMEM],
        out_specs=(VMEM, VMEM),
        compiler_params=SMALL,
        name="turn",
    )(scaled)


def match_kernel(obs_ref, pattern_ref, partner_ref, slot_ref):
    row, col = lax.axis_index("row"), lax.axis_index("col")

    def clear(k, unused):
        slot_ref[k] = SLOTS
        return unused

    def enter(q, unused):
        for b in range(2):
            slot_ref[b * NOBS + obs_ref[2 * col + b, q]] = q
        return unused

    def find(p, unused):
        for a in range(4):
            obs = obs_ref[row // 2 * 4 + a, p]
            for b in range(2):
                partner_ref[(a * SLOTS + p) * 2 + b] = slot_ref[b * NOBS + obs]
        return unused

    for a in range(4):
        for b in range(2):
            block_row, block_col = row // 2 * 4 + a, 2 * col + b
            low, high = jnp.minimum(block_row, block_col), jnp.maximum(block_row, block_col)
            partner_ref[8 * SLOTS + 2 * a + b] = pattern_ref[low, high]
    lax.fori_loop(0, 2 * NOBS, clear, 0, unroll=8)
    lax.fori_loop(0, SLOTS, enter, 0, unroll=4)
    lax.fori_loop(0, SLOTS, find, 0, unroll=4)


def match(obs_of, pattern):
    return pl.pallas_call(
        match_kernel,
        out_shape=jax.ShapeDtypeStruct((8 * SLOTS + 8,), jnp.int32),
        in_specs=[SMEM, SMEM],
        out_specs=SMEM,
        scratch_shapes=[pltpu.SMEM((2 * NOBS,), jnp.int32)],
        name="match",
    )(obs_of, pattern)


def pick_kernel(both_ref, out_ref):
    out_ref[...] = both_ref[lax.axis_index("col") % 2]


def pick(both):
    return pl.pallas_call(
        pick_kernel,
        out_shape=jax.ShapeDtypeStruct(both.shape[1:], both.dtype),
        in_specs=[VMEM],
        out_specs=VMEM,
        compiler_params=SMALL,
        name="pick",
    )(both)


def join_kernel(order, first_ref, second_ref, out_ref):
    at = 0
    if order == "core":
        at = lax.axis_index("col") % 2
    elif order == "y_low":
        at = lax.axis_index("row") % 2
    out_ref[at] = first_ref[...]
    out_ref[1 - at] = second_ref[...]


def join(first, second, order=None):
    return pl.pallas_call(
        functools.partial(join_kernel, order),
        out_shape=jax.ShapeDtypeStruct((2, *first.shape), first.dtype),
        in_specs=[VMEM, VMEM],
        out_specs=VMEM,
        compiler_params=SMALL,
        name="join",
    )(first, second)


def displaced(offset):
    steps, half = jnp.int32(0), jnp.int32(0)
    for at, (dx, dy) in DISPLACED.items():
        steps = jnp.where(offset == at, dx, steps)
        half = jnp.where(offset == at, dy, half)
    return steps, half


def multiply(group, partner_ref, row_refs, cols_ref, out_ref, prior_ref=None):
    col = lax.axis_index("col")
    y_high, x, core = col // 8, (col // 2) % 4, col % 2
    for a in range(2):
        total = jnp.zeros((BS, 2 * BS), jnp.float32)
        for k in range(8):
            source_x = (x + (0, 3, 1, 2)[k % 4]) % NX
            source_core = core if k < 4 else 1 - core
            lefts, rights = [], []
            for sub in range(2):
                source_y = y_high if sub == 0 else 1 - y_high
                slot = (source_y * 8 + source_x * 2 + source_core) * 2
                lefts.append(row_refs[k][sub, group, a])
                for s in range(2):
                    at = ((group * 2 + a) * SLOTS + slot + s) * 2
                    blocks = [cols_ref[b, partner_ref[at + b]] for b in range(2)]
                    rights.append(jnp.concatenate(blocks, axis=1))
            left, right = jnp.concatenate(lefts, axis=1), jnp.concatenate(rights, axis=0)
            total = total + jnp.dot(left, right, preferred_element_type=jnp.float32)
        for b in range(2):
            kept = partner_ref[8 * SLOTS + 2 * (group * 2 + a) + b] == 1
            at = slice(a * BS, (a + 1) * BS), slice(b * BS, (b + 1) * BS)
            part = total[:, b * BS : (b + 1) * BS]
            part = jnp.where(kept, part, jnp.zeros_like(part))
            out_ref[at] = part if prior_ref is None else prior_ref[at] + part


def give_kernel(partner_ref, *refs):
    row_refs, col_refs = refs[:8], refs[8:16]
    out_ref, cols_ref = refs[16:]
    row, col = lax.axis_index("row"), lax.axis_index("col")
    z, y_low = row // 2, row % 2
    y_high, x, core = col // 8, (col // 2) % 4, col % 2
    for b in range(2):
        cols_ref[b, SLOTS] = jnp.zeros((HALF, BS), jnp.bfloat16)
    way = 1 - 2 * core
    for ref, step in zip(col_refs, PIECES):
        steps, half = displaced((z + step * way - col // 2 + 2 * NZ) % NZ)
        source = (y_high + half) % 2 * 8 + (x - steps + NX) % NX * 2
        for cross in range(2):
            slot = 2 * (source + (y_low if cross == 0 else 1 - y_low))
            for b in range(2):
                for s in range(2):
                    cols_ref[b, slot + s] = ref[core, cross, b, s] if len(ref.shape) == 6 else ref[cross, b, s]
    multiply(1 - y_low, partner_ref, row_refs, cols_ref, out_ref)


def keep_kernel(partner_ref, *refs):
    row_refs = refs[:8]
    cols_ref, prior_ref, out_ref = refs[8:]
    group = lax.axis_index("row") % 2
    multiply(group, partner_ref, row_refs, cols_ref, out_ref, prior_ref)


TILE = jax.ShapeDtypeStruct((2 * BS, 2 * BS), jnp.float32)
COLS = jax.ShapeDtypeStruct((2, SLOTS + 1, HALF, BS), jnp.bfloat16)


def local(kernel, out_shape, smalls, arrays):
    many = isinstance(out_shape, tuple)
    return pl.pallas_call(
        kernel,
        out_shape=out_shape,
        in_specs=[SMEM] * len(smalls) + [VMEM] * len(arrays),
        out_specs=(VMEM,) * len(out_shape) if many else VMEM,
        compiler_params=pltpu.CompilerParams(vmem_limit_bytes=12 * 2**20),
    )(*smalls, *arrays)


def on_device(panels, obs_of, counts, inv_var, pattern, prior):
    scaled, same, cross = scale(obs_of, counts, inv_var, panels)
    mine = shift(same, SPREAD[0]), shift(cross, SPREAD[1])
    keep_t, give_t = turn(scaled)
    partner = match(obs_of, pattern)
    part = join(keep_t, shift(give_t, OTHER_Y), "y_low")
    part = join(part, shift(part, moves(dy=2)))
    row_pieces = [part, shift(part, moves(dx=1)), shift(part, moves(dx=-1)), shift(part, moves(dx=2))]
    row_pieces += [shift(piece, OTHER_CORE) for piece in row_pieces]
    own = join(*mine)
    ring = join(own, shift(own, OTHER_CORE), "core")
    col_pieces = [ring]
    for _ in range(1, 4):
        ring = shift(ring, RING)
        col_pieces += [ring, shift(ring, OTHER_CORE)]
    col_pieces.append(shift(pick(ring), RING))
    smalls = [partner]
    give, cols = local(give_kernel, (TILE, COLS), smalls, row_pieces + col_pieces)
    taken = shift(give, OTHER_Y)
    keep = local(keep_kernel, TILE, smalls, row_pieces + [cols, prior])
    return keep + taken


OTHER_CORE, OTHER_Y = moves(flip_core=1), moves(flip_y=1)


def solution(mesh):
    placed = (P("row", "col", None, None), P(), P(), P(), P(), P("row", "col"))
    return jax.shard_map(
        on_device, mesh=mesh, in_specs=placed, out_specs=P("row", "col"), check_vma=False
    )
```
